32 devices in a mesh: layer: 4 (over z), feat: 8 (over y, x, core).
Axes of the slice: x: 2, y: 2, z: 4, core: 2. Of those that a mesh axis runs over, the one named last changes fastest.
Arguments:
- sources: bfloat16 [4, 1024, 2304], P('layer', 'feat'), may hold values from -6 to 6
- w_encode: bfloat16 [4, 2304, 16384], P('layer', None, 'feat'), may hold values from -0.125 to 0.125
- b_encode: float32 [4, 16384], P('layer', 'feat'), may hold values from -3 to 3
- w_decode: bfloat16 [4, 16384, 2304], P('layer', 'feat'), may hold values from -0.046875 to 0.046875
- b_decode: float32 [2304], replicated, may hold values from -3 to 3
- target: bfloat16 [1024, 2304], replicated, may hold values from -6 to 6
Outputs:
- error: float32 [1024, 2304], P(('layer', 'feat'))
- feature_grad: bfloat16 [4, 1024, 16384], P('layer', None, 'feat')
- decoder_grad: bfloat16 [4, 16384, 2304], P('layer', 'feat')
The draws below stay inside these ranges and needn't reach their ends.
All inputs are finite; a program needn't handle non-finite values.
Results may differ from the reference program's by a relative error of at most 0.0056.
Values may be sent and summed in bfloat16 or wider, within the bound.
A program may use at most 128 MiB of HBM per device.

```python
import math
import jax
import jax.numpy as jnp
from jax import lax

D = 2304
F = 16384
TOKENS = 1024
LAYERS = 4


def block_scale(stream_key, dims, shards, smallest, high):
    factor_of, own = 1.0, jax.random.fold_in(stream_key, 6)
    for position, parts in shards:
        steps = jnp.exp(jax.random.uniform(jax.random.fold_in(own, position), (parts,), jnp.float32, smallest / len(shards), high / len(shards)))
        factor_of = factor_of * jnp.repeat(steps, dims[position] // parts).reshape([-1 if axis == position else 1 for axis in range(len(dims))])
    return factor_of


def noise(rng, dims, scale, most, pieces=(), held_as=jnp.bfloat16):
    drawn = scale * jax.random.normal(rng, dims, jnp.float32)
    if pieces:
        drawn = drawn * block_scale(rng, dims, pieces, -0.22, 0.18)
    return jnp.clip(drawn, -most, most).astype(held_as)


def setup_inputs(seed: int = 0) -> dict:
    seeds = jax.random.split(jax.random.key(seed), 7)
    sources = noise(seeds[0], (LAYERS, TOKENS, D), 1.0, 6.0, ((0, 4), (1, 8)))
    w_encode = noise(seeds[1], (LAYERS, D, F), D ** -0.5, 0.125, ((0, 4), (2, 8)))
    b_encode = noise(seeds[2], (LAYERS, F), 0.5, 3.0, ((0, 4), (1, 8)), jnp.float32)
    w_decode = noise(seeds[3], (LAYERS, F, D), F ** -0.5, 0.046875, ((0, 4), (1, 8)))
    b_decode = noise(seeds[4], (D,), 0.5, 3.0, (), jnp.float32)
    target = noise(seeds[5], (TOKENS, D), 1.0, 6.0)
    return {"sources": sources, "w_encode": w_encode, "b_encode": b_encode, "w_decode": w_decode, "b_decode": b_decode, "target": target}


def reference(sources, w_encode, b_encode, w_decode, b_decode, target):
    scale = 1.0 / math.sqrt(TOKENS)
    recon = jnp.zeros((TOKENS, D), jnp.float32)
    acts_list = []
    for layer_index in range(LAYERS):
        pre = jnp.dot(sources[layer_index], w_encode[layer_index], preferred_element_type=jnp.float32) + b_encode[layer_index]
        acts = jnp.maximum(pre, 0.0).astype(jnp.bfloat16)
        acts_list.append(acts)
        recon = recon + jnp.dot(acts, w_decode[layer_index], preferred_element_type=jnp.float32)
    error = recon + b_decode - target.astype(jnp.float32)
    error_low = error.astype(jnp.bfloat16)
    feature_list = []
    decoder_list = []
    for layer_index in range(LAYERS):
        grad_feat = lax.dot_general(error_low, w_decode[layer_index], (((1,), (1,)), ((), ())), preferred_element_type=jnp.float32)
        feature_list.append(grad_feat.astype(jnp.bfloat16))
        grad_dec = lax.dot_general(acts_list[layer_index], error_low, (((0,), (0,)), ((), ())), preferred_element_type=jnp.float32)
        decoder_list.append((grad_dec * scale).astype(jnp.bfloat16))
    return (error, jnp.stack(feature_list), jnp.stack(decoder_list))
```

```python
import math

import jax
import jax.numpy as jnp
from jax import lax
from jax.sharding import PartitionSpec as P

CHUNKS = 2
GROUP = ("layer", "feat")


def body(sources, w_encode, b_encode, w_decode, b_decode, target):
    encoder, bias, decoder = w_encode[0], b_encode[0], w_decode[0]
    dim = encoder.shape[0]
    tokens = target.shape[0]
    scale = 1.0 / math.sqrt(tokens)
    groups = lax.axis_size("layer") * lax.axis_size("feat")
    rows = tokens // groups
    part = rows // CHUNKS
    own = lax.axis_index("layer") * lax.axis_size("feat") + lax.axis_index("feat")
    held = sources[0].reshape(-1, CHUNKS, part, dim)
    acts, partial = [], []
    for c in range(CHUNKS):
        mine = held[:, c].reshape(-1, dim)
        tok = lax.all_gather(mine, "feat", axis=0, tiled=True)
        pre = jnp.dot(tok, encoder, preferred_element_type=jnp.float32) + bias
        acts.append(jnp.maximum(pre, 0.0).astype(jnp.bfloat16))
    own_target = lax.dynamic_slice_in_dim(target, own * rows, rows, 0).astype(jnp.float32)
    own_target = own_target.reshape(CHUNKS, part, dim)
    errors, lows = [], []
    for c in range(CHUNKS):
        p = jnp.dot(acts[c], decoder, preferred_element_type=jnp.float32).astype(jnp.bfloat16)
        s = lax.psum_scatter(p, GROUP, scatter_dimension=0, tiled=True)
        e = s.astype(jnp.float32) + b_decode - own_target[c]
        errors.append(e)
        lows.append(lax.all_gather(e.astype(jnp.bfloat16), GROUP, axis=0, tiled=True))
    error_out = jnp.concatenate(errors, 0)
    fgs = []
    for c in range(CHUNKS):
        fg = lax.dot_general(lows[c], decoder, (((1,), (1,)), ((), ())), preferred_element_type=jnp.float32)
        fgs.append(fg.astype(jnp.bfloat16).reshape(groups, 1, part, -1))
    feature_grad = jnp.concatenate(fgs, 1).reshape(1, tokens, -1)
    a = jnp.concatenate(acts, 0)
    l = jnp.concatenate(lows, 0)
    gd = lax.dot_general(a, l, (((0,), (0,)), ((), ())), preferred_element_type=jnp.float32)
    decoder_grad = (gd * scale).astype(jnp.bfloat16)[None]
    return (error_out, feature_grad, decoder_grad)


def solution(mesh):
    placed = (
        P("layer", "feat", None),
        P("layer", None, "feat"),
        P("layer", "feat"),
        P("layer", "feat", None),
        P(),
        P(),
    )
    return jax.shard_map(
        body,
        mesh=mesh,
        in_specs=placed,
        out_specs=(P(("layer", "feat"), None), P("layer", None, "feat"), P("layer", "feat", None)),
        check_vma=False,
    )
```

```python
import functools
import math

import jax
import jax.numpy as jnp
from jax import lax
from jax.experimental import pallas as pl
from jax.experimental.pallas import tpu as pltpu
from jax.sharding import PartitionSpec as P

MESH = pl.DeviceIdType.MESH
LIMIT = 60 * 1024 * 1024
PAIRS = 3


def whereami():
    f = lax.axis_index("feat")
    l = lax.axis_index("layer")
    c = f % 2
    x = (f // 2) % 2
    y = f // 4
    mate = f + 1 - 2 * c
    fx = f + 2 - 4 * x
    fy = f + 4 - 8 * y
    return l, f, c, x, y, mate, fx, fy


def greet(devices):
    barrier = pltpu.get_barrier_semaphore()
    for dev in devices:
        pl.semaphore_signal(barrier, inc=1, device_id=dev, device_id_type=MESH)
    pl.semaphore_wait(barrier, len(devices))


def encode_kernel(x_ref, enc_hbm, bias_ref, acts_ref, g, enc, send, recv, local):
    l, f, c, x, y, mate, fx, fy = whereami()
    fd = fx + fy - f
    rows = x_ref.shape[0]
    half = rows // 2
    load = pltpu.make_async_copy(enc_hbm, enc, local.at[0])
    load.start()
    keep = pltpu.make_async_copy(x_ref, g.at[f], local.at[1])
    keep.start()
    greet([(l, mate), (l, fx), (l, fy)])

    def push(i, src, dst, to):
        copy = pltpu.make_async_remote_copy(
            src_ref=src, dst_ref=dst, send_sem=send.at[i], recv_sem=recv.at[i],
            device_id=(l, to), device_id_type=MESH)
        copy.start()
        return copy

    def compute(first):
        base = first - c
        width = 512 if enc.shape[1] % 512 == 0 else enc.shape[1]

        def step(i, carry):
            cols = pl.ds(pl.multiple_of(i * width, width), width)
            tok = g[pl.ds(base, 2)].reshape(2 * rows, g.shape[2])
            pre = jnp.dot(tok, enc[:, cols], preferred_element_type=jnp.float32)
            pre = pre + bias_ref[:, cols]
            acts_ref[pl.ds(pl.multiple_of(base * rows, 2 * rows), 2 * rows), cols] = (
                jnp.maximum(pre, 0.0).astype(acts_ref.dtype))
            return carry

        lax.fori_loop(0, enc.shape[1] // width, step, 0)

    s1 = push(1, x_ref, g.at[f], fx)
    s2 = push(2, x_ref, g.at[f], fy)
    s0 = push(0, x_ref, g.at[f], mate)
    keep.wait()
    load.wait()
    s0.wait_recv()
    compute(f)
    s1.wait_recv()
    s4 = push(4, g.at[fx, pl.ds(0, half)], g.at[fx, pl.ds(0, half)], fy)
    s3 = push(3, g.at[fx], g.at[fx], mate)
    s2.wait_recv()
    s6 = push(6, g.at[fy, pl.ds(half, half)], g.at[fy, pl.ds(half, half)], fx)
    s5 = push(5, g.at[fy], g.at[fy], mate)
    s3.wait_recv()
    compute(fx)
    s5.wait_recv()
    compute(fy)
    s4.wait_recv()
    s6.wait_recv()
    s7 = push(7, g.at[fd], g.at[fd], mate)
    s7.wait_recv()
    compute(fd)
    for s in (s0, s1, s2, s3, s4, s5, s6, s7):
        s.wait_send()


def reduce_kernel(layers, acts_hbm, dec_hbm, bias_ref, target_hbm, err_ref, low_hbm,
                  acts, dec, tgt, p, rc, r1, r2, rz, e, send, recv, zsend, zrecv, local):
    l, f, c, x, y, mate, fx, fy = whereami()
    rows, width = p.shape[-2:]
    feats = 8
    span = feats * rows
    own = l * feats + f
    loads = [
        pltpu.make_async_copy(acts_hbm, acts, local.at[0]),
        pltpu.make_async_copy(dec_hbm, dec, local.at[1]),
        pltpu.make_async_copy(
            target_hbm.at[pl.ds(pl.multiple_of(own * rows, rows), rows)], tgt, local.at[2]),
    ]
    for load in loads:
        load.start()
    peers = [(l + dz) % layers for dz in range(1, layers)]
    greet([(l, mate), (l, fx), (l, fy)] + [(q, f) for q in peers])
    for load in loads:
        load.wait()
    live = {}

    def push(key, j, src, dst, to):
        copy = pltpu.make_async_remote_copy(
            src_ref=src, dst_ref=dst, send_sem=send.at[key, j], recv_sem=recv.at[key, j],
            device_id=(l, to), device_id_type=MESH)
        copy.start()
        live[key, j] = copy

    def zpush(key, j, n, src, dst):
        copy = pltpu.make_async_remote_copy(
            src_ref=src, dst_ref=dst, send_sem=zsend.at[key, j, n], recv_sem=zrecv.at[key, j, n],
            device_id=(peers[n], f), device_id_type=MESH)
        copy.start()
        live[key, j, n] = copy

    def add(a, b):
        return (a.astype(jnp.float32) + b.astype(jnp.float32)).astype(p.dtype)

    def multiply(pair):
        cols = pl.ds(pair * 2 * width, 2 * width)

        def step(i, carry):
            a = acts[pl.ds(pl.multiple_of(i * span, span), span), :]
            out = jnp.dot(a, dec[:, cols], preferred_element_type=jnp.float32).astype(p.dtype)
            for k in range(feats):
                for h in range(2):
                    p[2 * pair + h, k % 2, k // 4, (k // 2) % 2, i] = (
                        out[k * rows:(k + 1) * rows, h * width:(h + 1) * width])
            return carry

        lax.fori_loop(0, layers, step, 0)

    def stage(s, j):
        flip = j % 2
        if s == 0:
            push(0, j, p.at[j, 1 - c], rc.at[j], mate)
        elif s == 1:
            live[0, j].wait_recv()
            for yy in range(2):
                for xx in range(2):
                    p[j, c, yy, xx] = add(p[j, c, yy, xx], rc[j, yy, xx])
            if flip:
                push(1, j, p.at[j, c, 1 - y], r1.at[j], fy)
            else:
                push(1, j, p.at[j, c, :, 1 - x], r1.at[j], fx)
        elif s == 2:
            live[1, j].wait_recv()
            for t in range(2):
                if flip:
                    p[j, c, y, t] = add(p[j, c, y, t], r1[j, t])
                else:
                    p[j, c, t, x] = add(p[j, c, t, x], r1[j, t])
            if flip:
                push(2, j, p.at[j, c, y, 1 - x], r2.at[j], fx)
            else:
                push(2, j, p.at[j, c, 1 - y, x], r2.at[j], fy)
        elif s == 3:
            live[2, j].wait_recv()
            p[j, c, y, x] = add(p[j, c, y, x], r2[j])
            for n, q in enumerate(peers):
                zpush(0, j, n, p.at[j, c, y, x, q], rz.at[j, n])
        elif s == 4:
            total = p[j, c, y, x, l].astype(jnp.float32)
            for n in range(layers - 1):
                live[0, j, n].wait_recv()
                total = total + rz[j, n].astype(jnp.float32)
            cols = pl.ds(j * width, width)
            total = total + bias_ref[:, cols] - tgt[:, cols].astype(jnp.float32)
            err_ref[:, cols] = total
            e[j, l, y, x, c] = total.astype(e.dtype)
            for n in range(layers - 1):
                zpush(1, j, n, e.at[j, l, y, x, c], e.at[j, l, y, x, c])
        elif s == 5:
            for n in range(layers - 1):
                live[1, j, n].wait_recv()
            ref = e.at[j, :, y, x, c]
            push(3, j, ref, ref, fy if flip else fx)
        elif s == 6:
            live[3, j].wait_recv()
            ref = e.at[j, :, :, x, c] if flip else e.at[j, :, y, :, c]
            push(4, j, ref, ref, fx if flip else fy)
        elif s == 7:
            live[4, j].wait_recv()
            ref = e.at[j, :, :, :, c]
            push(5, j, ref, ref, mate)
        elif s == 8:
            live[5, j].wait_recv()
            out = pltpu.make_async_copy(
                e.at[j], low_hbm.at[:, :, :, :, :, pl.ds(j * width, width)], local.at[3 + j])
            out.start()
            live["out", j] = out

    for t in range(PAIRS + 8):
        for pair in range(PAIRS):
            s = t - pair
            if 0 <= s <= 8:
                if s == 0:
                    multiply(pair)
                for h in range(2):
                    stage(s, 2 * pair + h)
    for key, copy in live.items():
        if key[0] == "out":
            copy.wait()
        else:
            copy.wait_send()


def body(layers, sources, w_encode, b_encode, w_decode, b_decode, target):
    encoder, bias, decoder = w_encode[0], b_encode, w_decode[0]
    dim, feats_dev = encoder.shape
    tokens = target.shape[0]
    scale = 1.0 / math.sqrt(tokens)
    shard = sources.shape[1]
    rows = tokens // (layers * 8)
    width = dim // (2 * PAIRS)
    chunks = 2 * PAIRS
    vmem = pl.BlockSpec(memory_space=pltpu.VMEM)
    any_ = pl.BlockSpec(memory_space=pl.ANY)
    bf = jnp.bfloat16
    dma = pltpu.SemaphoreType.DMA
    acts = pl.pallas_call(
        encode_kernel,
        out_shape=jax.ShapeDtypeStruct((tokens, feats_dev), bf),
        in_specs=[vmem, any_, vmem],
        out_specs=vmem,
        scratch_shapes=[
            pltpu.VMEM((8, shard, dim), bf), pltpu.VMEM((dim, feats_dev), bf),
            dma((8,)), dma((8,)), dma((2,)),
        ],
        compiler_params=pltpu.CompilerParams(
            collective_id=0, has_side_effects=True, vmem_limit_bytes=LIMIT),
    )(sources[0], encoder, bias)
    error_out, low = pl.pallas_call(
        functools.partial(reduce_kernel, layers),
        out_shape=(
            jax.ShapeDtypeStruct((rows, dim), jnp.float32),
            jax.ShapeDtypeStruct((layers, 2, 2, 2, rows, dim), bf),
        ),
        in_specs=[any_, any_, vmem, any_],
        out_specs=(vmem, any_),
        scratch_shapes=[
            pltpu.VMEM((tokens, feats_dev), bf),
            pltpu.VMEM((feats_dev, dim), bf),
            pltpu.VMEM((rows, dim), bf),
            pltpu.VMEM((chunks, 2, 2, 2, layers, rows, width), bf),
            pltpu.VMEM((chunks, 2, 2, layers, rows, width), bf),
            pltpu.VMEM((chunks, 2, layers, rows, width), bf),
            pltpu.VMEM((chunks, layers, rows, width), bf),
            pltpu.VMEM((chunks, layers - 1, rows, width), bf),
            pltpu.VMEM((chunks, layers, 2, 2, 2, rows, width), bf),
            dma((6, chunks)), dma((6, chunks)),
            dma((2, chunks, layers - 1)), dma((2, chunks, layers - 1)),
            dma((3 + chunks,)),
        ],
        compiler_params=pltpu.CompilerParams(
            collective_id=1, has_side_effects=True, vmem_limit_bytes=LIMIT),
    )(acts, decoder, b_decode[None], target)
    low = low.reshape(tokens, dim)
    grad_feat = lax.dot_general(
        low, decoder, (((1,), (1,)), ((), ())), preferred_element_type=jnp.float32)
    grad_dec = lax.dot_general(
        acts, low, (((0,), (0,)), ((), ())), preferred_element_type=jnp.float32)
    return (error_out, grad_feat.astype(bf)[None], (grad_dec * scale).astype(bf)[None])


def plain(sources, w_encode, b_encode, w_decode, b_decode, target):
    tok = lax.all_gather(sources[0], "feat", axis=0, tiled=True)
    pre = jnp.dot(tok, w_encode[0], preferred_element_type=jnp.float32) + b_encode[0]
    acts = jnp.maximum(pre, 0.0).astype(jnp.bfloat16)
    tokens = acts.shape[0]
    decoder = w_decode[0]
    rows = tokens // (lax.axis_size("layer") * lax.axis_size("feat"))
    own = lax.axis_index("layer") * lax.axis_size("feat") + lax.axis_index("feat")
    total = lax.psum(jnp.dot(acts, decoder, preferred_element_type=jnp.float32), ("layer", "feat"))
    error = total + b_decode - target.astype(jnp.float32)
    low = error.astype(jnp.bfloat16)
    grad_feat = lax.dot_general(
        low, decoder, (((1,), (1,)), ((), ())), preferred_element_type=jnp.float32)
    grad_dec = lax.dot_general(
        acts, low, (((0,), (0,)), ((), ())), preferred_element_type=jnp.float32)
    grad_dec = grad_dec * (1.0 / math.sqrt(tokens))
    return (lax.dynamic_slice_in_dim(error, own * rows, rows, 0),
            grad_feat.astype(jnp.bfloat16)[None], grad_dec.astype(jnp.bfloat16)[None])


def solution(mesh):
    layers, feats = mesh.shape["layer"], mesh.shape["feat"]
    placed = (
        P("layer", "feat", None),
        P("layer", None, "feat"),
        P("layer", "feat"),
        P("layer", "feat", None),
        P(),
        P(),
    )

    def run(*args):
        tokens, dim = args[5].shape
        fits = feats == 8 and tokens % (layers * feats * 16) == 0 and dim % (PAIRS * 256) == 0
        chosen = functools.partial(body, layers) if fits else plain
        return jax.shard_map(
            chosen,
            mesh=mesh,
            in_specs=placed,
            out_specs=(P(("layer", "feat"), None), P("layer", None, "feat"),
                       P("layer", "feat", None)),
            check_vma=False,
        )(*args)

    return run
```

```python
import functools
import math

import jax
import jax.numpy as jnp
from jax import lax
from jax.experimental import pallas as pl
from jax.experimental.pallas import tpu as pltpu
from jax.sharding import PartitionSpec as P

MESH = pl.DeviceIdType.MESH
LIMIT = 60 * 1024 * 1024
PAIRS = 3


def whereami():
    f = lax.axis_index("feat")
    l = lax.axis_index("layer")
    c = f % 2
    x = (f // 2) % 2
    y = f // 4
    mate = f + 1 - 2 * c
    fx = f + 2 - 4 * x
    fy = f + 4 - 8 * y
    return l, f, c, x, y, mate, fx, fy


def greet(devices):
    barrier = pltpu.get_barrier_semaphore()
    for dev in devices:
        pl.semaphore_signal(barrier, inc=1, device_id=dev, device_id_type=MESH)
    pl.semaphore_wait(barrier, len(devices))


def fused_kernel(layers, x_ref, enc_hbm, ebias_ref, dec_hbm, bias_ref, target_hbm,
                 err_ref, acts_hbm, low_hbm,
                 g, enc, acts, dec, tgt, p, rc, r1, r2, rz, e,
                 gsend, grecv, bsend, brecv, send, recv, zsend, zrecv, local):
    l, f, c, x, y, mate, fx, fy = whereami()
    fd = fx + fy - f
    rows, width = p.shape[-2:]
    feats = 8
    span = feats * rows
    own = l * feats + f
    shard = x_ref.shape[0]
    half = shard // 2
    pair_rows = 2 * shard
    load_enc = pltpu.make_async_copy(enc_hbm, enc, local.at[0])
    load_dec = pltpu.make_async_copy(dec_hbm, dec, local.at[1])
    load_tgt = pltpu.make_async_copy(
        target_hbm.at[pl.ds(pl.multiple_of(own * rows, rows), rows)], tgt, local.at[2])
    keep = pltpu.make_async_copy(x_ref, g.at[f], local.at[3])
    load_enc.start()
    keep.start()
    peers = [(l + dz) % layers for dz in range(1, layers)]
    greet([(l, mate), (l, fx), (l, fy)] + [(q, f) for q in peers])
    live = {}

    def gpush(i, src, dst, to):
        copy = pltpu.make_async_remote_copy(
            src_ref=src, dst_ref=dst, send_sem=gsend.at[i], recv_sem=grecv.at[i],
            device_id=(l, to), device_id_type=MESH)
        copy.start()
        return copy

    s1 = gpush(1, x_ref, g.at[f], fx)
    s2 = gpush(2, x_ref, g.at[f], fy)
    s0 = gpush(0, x_ref, g.at[f], mate)
    load_dec.start()
    load_tgt.start()

    def push(key, j, src, dst, to):
        copy = pltpu.make_async_remote_copy(
            src_ref=src, dst_ref=dst, send_sem=send.at[key, j], recv_sem=recv.at[key, j],
            device_id=(l, to), device_id_type=MESH)
        copy.start()
        live[key, j] = copy

    def zpush(key, j, n, src, dst):
        copy = pltpu.make_async_remote_copy(
            src_ref=src, dst_ref=dst, send_sem=zsend.at[key, j, n], recv_sem=zrecv.at[key, j, n],
            device_id=(peers[n], f), device_id_type=MESH)
        copy.start()
        live[key, j, n] = copy

    def add(a, b):
        return (a.astype(jnp.float32) + b.astype(jnp.float32)).astype(p.dtype)

    def encode(first):
        base = first - c
        wide = 512 if enc.shape[1] % 512 == 0 else enc.shape[1]

        def step(i, carry):
            cols = pl.ds(pl.multiple_of(i * wide, wide), wide)
            tok = g[pl.ds(base, 2)].reshape(pair_rows, g.shape[2])
            pre = jnp.dot(tok, enc[:, cols], preferred_element_type=jnp.float32)
            pre = pre + ebias_ref[:, cols]
            acts[pl.ds(pl.multiple_of(base * shard, pair_rows), pair_rows), cols] = (
                jnp.maximum(pre, 0.0).astype(acts.dtype))
            return carry

        lax.fori_loop(0, enc.shape[1] // wide, step, 0)
        out = pltpu.make_async_copy(
            acts.at[pl.ds(pl.multiple_of(base * shard, pair_rows), pair_rows)],
            acts_hbm.at[pl.ds(pl.multiple_of(base * shard, pair_rows), pair_rows)],
            local.at[4 + len(stores)])
        out.start()
        stores.append(out)

    def multiply(first, pair):
        base = first - c
        i = first // 2
        a = acts[pl.ds(pl.multiple_of(base * shard, pair_rows), pair_rows), :]
        cols = pl.ds(pl.multiple_of(pair * 2 * width, 2 * width), 2 * width)
        out = jnp.dot(a, dec[:, cols], preferred_element_type=jnp.float32).astype(p.dtype)
        for k in range(feats):
            for h in range(2):
                p[2 * pair + h, k % 2, k // 4, (k // 2) % 2, i] = (
                    out[k * rows:(k + 1) * rows, h * width:(h + 1) * width])

    def block(first, order):
        encode(first)
        if order == 0:
            load_dec.wait()
            load_tgt.wait()

        def step(pair, carry):
            multiply(first, pair)
            return carry

        lax.fori_loop(0, PAIRS, step, 0)
        i = first // 2
        copy = pltpu.make_async_remote_copy(
            src_ref=p.at[:, 1 - c, :, :, i], dst_ref=rc.at[:, :, :, i],
            send_sem=bsend.at[order], recv_sem=brecv.at[order],
            device_id=(l, mate), device_id_type=MESH)
        copy.start()
        early.append(copy)

    stores, early = [], []

    def stage(s, j):
        flip = j % 2
        if s == 0:
            push(0, j, p.at[j, 1 - c, :, :, fd // 2], rc.at[j, :, :, fd // 2], mate)
        elif s == 1:
            live[0, j].wait_recv()
            for yy in range(2):
                for xx in range(2):
                    p[j, c, yy, xx] = add(p[j, c, yy, xx], rc[j, yy, xx])
            if flip:
                push(1, j, p.at[j, c, 1 - y], r1.at[j], fy)
            else:
                push(1, j, p.at[j, c, :, 1 - x], r1.at[j], fx)
        elif s == 2:
            live[1, j].wait_recv()
            for t in range(2):
                if flip:
                    p[j, c, y, t] = add(p[j, c, y, t], r1[j, t])
                else:
                    p[j, c, t, x] = add(p[j, c, t, x], r1[j, t])
            if flip:
                push(2, j, p.at[j, c, y, 1 - x], r2.at[j], fx)
            else:
                push(2, j, p.at[j, c, 1 - y, x], r2.at[j], fy)
        elif s == 3:
            live[2, j].wait_recv()
            p[j, c, y, x] = add(p[j, c, y, x], r2[j])
            for n, q in enumerate(peers):
                zpush(0, j, n, p.at[j, c, y, x, q], rz.at[j, n])
        elif s == 4:
            total = p[j, c, y, x, l].astype(jnp.float32)
            for n in range(layers - 1):
                live[0, j, n].wait_recv()
                total = total + rz[j, n].astype(jnp.float32)
            cols = pl.ds(j * width, width)
            total = total + bias_ref[:, cols] - tgt[:, cols].astype(jnp.float32)
            err_ref[:, cols] = total
            e[j, l, y, x, c] = total.astype(e.dtype)
            for n in range(layers - 1):
                zpush(1, j, n, e.at[j, l, y, x, c], e.at[j, l, y, x, c])
        elif s == 5:
            for n in range(layers - 1):
                live[1, j, n].wait_recv()
            ref = e.at[j, :, y, x, c]
            push(3, j, ref, ref, fy if flip else fx)
        elif s == 6:
            live[3, j].wait_recv()
            ref = e.at[j, :, :, x, c] if flip else e.at[j, :, y, :, c]
            push(4, j, ref, ref, fx if flip else fy)
        elif s == 7:
            live[4, j].wait_recv()
            ref = e.at[j, :, :, :, c]
            push(5, j, ref, ref, mate)
        elif s == 8:
            live[5, j].wait_recv()
            out = pltpu.make_async_copy(
                e.at[j], low_hbm.at[:, :, :, :, :, pl.ds(j * width, width)], local.at[8 + j])
            out.start()
            live["out", j] = out

    keep.wait()
    load_enc.wait()
    s0.wait_recv()
    block(f, 0)
    s1.wait_recv()
    s4 = gpush(4, g.at[fx, pl.ds(0, half)], g.at[fx, pl.ds(0, half)], fy)
    s3 = gpush(3, g.at[fx], g.at[fx], mate)
    s2.wait_recv()
    s6 = gpush(6, g.at[fy, pl.ds(half, half)], g.at[fy, pl.ds(half, half)], fx)
    s5 = gpush(5, g.at[fy], g.at[fy], mate)
    s3.wait_recv()
    block(fx, 1)
    s4.wait_recv()
    s6.wait_recv()
    s7 = gpush(7, g.at[fd], g.at[fd], mate)
    s5.wait_recv()
    block(fy, 2)
    s7.wait_recv()
    encode(fd)
    for copy in early:
        copy.wait_recv()
    for t in range(PAIRS + 8):
        for pair in range(PAIRS):
            s = t - pair
            if 0 <= s <= 8:
                if s == 0:
                    multiply(fd, pair)
                for h in range(2):
                    stage(s, 2 * pair + h)
    for copy in stores:
        copy.wait()
    for copy in [s0, s1, s2, s3, s4, s5, s6, s7] + early:
        copy.wait_send()
    for key, copy in live.items():
        if key[0] == "out":
            copy.wait()
        else:
            copy.wait_send()


def body(layers, sources, w_encode, b_encode, w_decode, b_decode, target):
    encoder, bias, decoder = w_encode[0], b_encode, w_decode[0]
    dim, feats_dev = encoder.shape
    tokens = target.shape[0]
    scale = 1.0 / math.sqrt(tokens)
    shard = sources.shape[1]
    rows = tokens // (layers * 8)
    width = dim // (2 * PAIRS)
    chunks = 2 * PAIRS
    vmem = pl.BlockSpec(memory_space=pltpu.VMEM)
    any_ = pl.BlockSpec(memory_space=pl.ANY)
    bf = jnp.bfloat16
    dma = pltpu.SemaphoreType.DMA
    error_out, acts, low = pl.pallas_call(
        functools.partial(fused_kernel, layers),
        out_shape=(
            jax.ShapeDtypeStruct((rows, dim), jnp.float32),
            jax.ShapeDtypeStruct((tokens, feats_dev), bf),
            jax.ShapeDtypeStruct((layers, 2, 2, 2, rows, dim), bf),
        ),
        in_specs=[vmem, any_, vmem, any_, vmem, any_],
        out_specs=(vmem, any_, any_),
        scratch_shapes=[
            pltpu.VMEM((8, shard, dim), bf),
            pltpu.VMEM((dim, feats_dev), bf),
            pltpu.VMEM((tokens, feats_dev), bf),
            pltpu.VMEM((feats_dev, dim), bf),
            pltpu.VMEM((rows, dim), bf),
            pltpu.VMEM((chunks, 2, 2, 2, layers, rows, width), bf),
            pltpu.VMEM((chunks, 2, 2, layers, rows, width), bf),
            pltpu.VMEM((chunks, 2, layers, rows, width), bf),
            pltpu.VMEM((chunks, layers, rows, width), bf),
            pltpu.VMEM((chunks, layers - 1, rows, width), bf),
            pltpu.VMEM((chunks, layers, 2, 2, 2, rows, width), bf),
            dma((8,)), dma((8,)), dma((3,)), dma((3,)),
            dma((6, chunks)), dma((6, chunks)),
            dma((2, chunks, layers - 1)), dma((2, chunks, layers - 1)),
            dma((8 + chunks,)),
        ],
        compiler_params=pltpu.CompilerParams(
            collective_id=0, has_side_effects=True, vmem_limit_bytes=LIMIT),
    )(sources[0], encoder, bias, decoder, b_decode[None], target)
    low = low.reshape(tokens, dim)
    grad_feat = lax.dot_general(
        low, decoder, (((1,), (1,)), ((), ())), preferred_element_type=jnp.float32)
    grad_dec = lax.dot_general(
        acts, low, (((0,), (0,)), ((), ())), preferred_element_type=jnp.float32)
    return (error_out, grad_feat.astype(bf)[None], (grad_dec * scale).astype(bf)[None])


def plain(sources, w_encode, b_encode, w_decode, b_decode, target):
    tok = lax.all_gather(sources[0], "feat", axis=0, tiled=True)
    pre = jnp.dot(tok, w_encode[0], preferred_element_type=jnp.float32) + b_encode[0]
    acts = jnp.maximum(pre, 0.0).astype(jnp.bfloat16)
    tokens = acts.shape[0]
    decoder = w_decode[0]
    rows = tokens // (lax.axis_size("layer") * lax.axis_size("feat"))
    own = lax.axis_index("layer") * lax.axis_size("feat") + lax.axis_index("feat")
    total = lax.psum(jnp.dot(acts, decoder, preferred_element_type=jnp.float32), ("layer", "feat"))
    error = total + b_decode - target.astype(jnp.float32)
    low = error.astype(jnp.bfloat16)
    grad_feat = lax.dot_general(
        low, decoder, (((1,), (1,)), ((), ())), preferred_element_type=jnp.float32)
    grad_dec = lax.dot_general(
        acts, low, (((0,), (0,)), ((), ())), preferred_element_type=jnp.float32)
    grad_dec = grad_dec * (1.0 / math.sqrt(tokens))
    return (lax.dynamic_slice_in_dim(error, own * rows, rows, 0),
            grad_feat.astype(jnp.bfloat16)[None], grad_dec.astype(jnp.bfloat16)[None])


def solution(mesh):
    layers, feats = mesh.shape["layer"], mesh.shape["feat"]
    placed = (
        P("layer", "feat", None),
        P("layer", None, "feat"),
        P("layer", "feat"),
        P("layer", "feat", None),
        P(),
        P(),
    )

    def run(*args):
        tokens, dim = args[5].shape
        fits = feats == 8 and layers == 4 and tokens % (layers * feats * 16) == 0 and dim % (PAIRS * 256) == 0
        chosen = functools.partial(body, layers) if fits else plain
        return jax.shard_map(
            chosen,
            mesh=mesh,
            in_specs=placed,
            out_specs=(P(("layer", "feat"), None), P("layer", None, "feat"),
                       P("layer", "feat", None)),
            check_vma=False,
        )(*args)

    return run
```

```python
import functools
import math

import jax
import jax.numpy as jnp
from jax import lax
from jax.experimental import pallas as pl
from jax.experimental.pallas import tpu as pltpu
from jax.sharding import PartitionSpec as P

MESH = pl.DeviceIdType.MESH
LIMIT = 60 * 1024 * 1024
PAIRS = 3


def whereami():
    f = lax.axis_index("feat")
    l = lax.axis_index("layer")
    c = f % 2
    x = (f // 2) % 2
    y = f // 4
    mate = f + 1 - 2 * c
    fx = f + 2 - 4 * x
    fy = f + 4 - 8 * y
    return l, f, c, x, y, mate, fx, fy


def greet(devices):
    barrier = pltpu.get_barrier_semaphore()
    for dev in devices:
        pl.semaphore_signal(barrier, inc=1, device_id=dev, device_id_type=MESH)
    pl.semaphore_wait(barrier, len(devices))


def fused_kernel(layers, x_ref, enc_hbm, ebias_ref, dec_hbm, bias_ref, target_hbm,
                 err_ref, acts_hbm, low_hbm,
                 g, enc, acts, dec, tgt, p, rc, r1, r2, rz, e,
                 gsend, grecv, bsend, brecv, send, recv, zsend, zrecv, local):
    l, f, c, x, y, mate, fx, fy = whereami()
    fd = fx + fy - f
    rows, width = p.shape[-2:]
    feats = 8
    span = feats * rows
    own = l * feats + f
    shard = x_ref.shape[0]
    half = shard // 2
    pair_rows = 2 * shard
    load_enc = pltpu.make_async_copy(enc_hbm, enc, local.at[0])
    load_dec = pltpu.make_async_copy(dec_hbm, dec, local.at[1])
    load_tgt = pltpu.make_async_copy(
        target_hbm.at[pl.ds(pl.multiple_of(own * rows, rows), rows)], tgt, local.at[2])
    keep = pltpu.make_async_copy(x_ref, g.at[f], local.at[3])
    load_enc.start()
    keep.start()
    peers = [(l + dz) % layers for dz in range(1, layers)]
    greet([(l, mate), (l, fx), (l, fy)] + [(q, f) for q in peers])
    live = {}

    def gpush(i, src, dst, to):
        copy = pltpu.make_async_remote_copy(
            src_ref=src, dst_ref=dst, send_sem=gsend.at[i], recv_sem=grecv.at[i],
            device_id=(l, to), device_id_type=MESH)
        copy.start()
        return copy

    s1 = gpush(1, x_ref, g.at[f], fx)
    s2 = gpush(2, x_ref, g.at[f], fy)
    s0 = gpush(0, x_ref, g.at[f], mate)
    load_dec.start()
    load_tgt.start()

    def push(key, j, src, dst, to):
        copy = pltpu.make_async_remote_copy(
            src_ref=src, dst_ref=dst, send_sem=send.at[key, j], recv_sem=recv.at[key, j],
            device_id=(l, to), device_id_type=MESH)
        copy.start()
        live[key, j] = copy

    def zpush(key, j, n, src, dst):
        copy = pltpu.make_async_remote_copy(
            src_ref=src, dst_ref=dst, send_sem=zsend.at[key, j, n], recv_sem=zrecv.at[key, j, n],
            device_id=(peers[n], f), device_id_type=MESH)
        copy.start()
        live[key, j, n] = copy

    def add(a, b):
        return (a.astype(jnp.float32) + b.astype(jnp.float32)).astype(p.dtype)

    def encode(first):
        base = first - c
        wide = 512 if enc.shape[1] % 512 == 0 else enc.shape[1]

        def step(i, carry):
            cols = pl.ds(pl.multiple_of(i * wide, wide), wide)
            tok = g[pl.ds(base, 2)].reshape(pair_rows, g.shape[2])
            pre = jnp.dot(tok, enc[:, cols], preferred_element_type=jnp.float32)
            pre = pre + ebias_ref[:, cols]
            acts[pl.ds(pl.multiple_of(base * shard, pair_rows), pair_rows), cols] = (
                jnp.maximum(pre, 0.0).astype(acts.dtype))
            return carry

        lax.fori_loop(0, enc.shape[1] // wide, step, 0)
        out = pltpu.make_async_copy(
            acts.at[pl.ds(pl.multiple_of(base * shard, pair_rows), pair_rows)],
            acts_hbm.at[pl.ds(pl.multiple_of(base * shard, pair_rows), pair_rows)],
            local.at[4 + len(stores)])
        out.start()
        stores.append(out)

    def multiply(first, pair):
        base = first - c
        i = first // 2
        a = acts[pl.ds(pl.multiple_of(base * shard, pair_rows), pair_rows), :]
        cols = pl.ds(pl.multiple_of(pair * 2 * width, 2 * width), 2 * width)
        out = jnp.dot(a, dec[:, cols], preferred_element_type=jnp.float32).astype(p.dtype)
        for k in range(feats):
            for h in range(2):
                p[2 * pair + h, k % 2, k // 4, (k // 2) % 2, i] = (
                    out[k * rows:(k + 1) * rows, h * width:(h + 1) * width])

    def block(first, order):
        encode(first)
        if order == 0:
            load_dec.wait()
            load_tgt.wait()

        def step(pair, carry):
            multiply(first, pair)
            return carry

        lax.fori_loop(0, PAIRS, step, 0)
        i = first // 2
        copy = pltpu.make_async_remote_copy(
            src_ref=p.at[:, 1 - c, :, :, i], dst_ref=rc.at[:, :, :, i],
            send_sem=bsend.at[order], recv_sem=brecv.at[order],
            device_id=(l, mate), device_id_type=MESH)
        copy.start()
        early.append(copy)

    stores, early = [], []

    def stage(s, j):
        flip = j % 2
        if s == 0:
            push(0, j, p.at[j, 1 - c, :, :, fd // 2], rc.at[j, :, :, fd // 2], mate)
        elif s == 1:
            live[0, j].wait_recv()
            for yy in range(2):
                for xx in range(2):
                    p[j, c, yy, xx] = add(p[j, c, yy, xx], rc[j, yy, xx])
            if flip:
                push(1, j, p.at[j, c, 1 - y], r1.at[j], fy)
            else:
                push(1, j, p.at[j, c, :, 1 - x], r1.at[j], fx)
        elif s == 2:
            live[1, j].wait_recv()
            for t in range(2):
                if flip:
                    p[j, c, y, t] = add(p[j, c, y, t], r1[j, t])
                else:
                    p[j, c, t, x] = add(p[j, c, t, x], r1[j, t])
            if flip:
                push(2, j, p.at[j, c, y, 1 - x], r2.at[j], fx)
            else:
                push(2, j, p.at[j, c, 1 - y, x], r2.at[j], fy)
        elif s == 3:
            live[2, j].wait_recv()
            p[j, c, y, x] = add(p[j, c, y, x], r2[j])
            for n, q in enumerate(peers):
                zpush(0, j, n, p.at[j, c, y, x, q], rz.at[j, n])
        elif s == 4:
            total = p[j, c, y, x, l].astype(jnp.float32)
            for n in range(layers - 1):
                live[0, j, n].wait_recv()
                total = total + rz[j, n].astype(jnp.float32)
            cols = pl.ds(j * width, width)
            total = total + bias_ref[cols].reshape(1, width) - tgt[:, cols].astype(jnp.float32)
            err_ref[:, cols] = total
            e[j, l, y, x, c] = total.astype(e.dtype)
            for n in range(layers - 1):
                zpush(1, j, n, e.at[j, l, y, x, c], e.at[j, l, y, x, c])
        elif s == 5:
            for n in range(layers - 1):
                live[1, j, n].wait_recv()
            ref = e.at[j, :, y, x, c]
            push(3, j, ref, ref, fy if flip else fx)
        elif s == 6:
            live[3, j].wait_recv()
            ref = e.at[j, :, :, x, c] if flip else e.at[j, :, y, :, c]
            push(4, j, ref, ref, fx if flip else fy)
        elif s == 7:
            live[4, j].wait_recv()
            ref = e.at[j, :, :, :, c]
            push(5, j, ref, ref, mate)
        elif s == 8:
            live[5, j].wait_recv()
            out = pltpu.make_async_copy(
                e.at[j], low_hbm.at[:, :, :, :, :, pl.ds(j * width, width)], local.at[8 + j])
            out.start()
            live["out", j] = out

    keep.wait()
    load_enc.wait()
    s0.wait_recv()
    block(f, 0)
    s1.wait_recv()
    s4 = gpush(4, g.at[fx, pl.ds(0, half)], g.at[fx, pl.ds(0, half)], fy)
    s3 = gpush(3, g.at[fx], g.at[fx], mate)
    s2.wait_recv()
    s6 = gpush(6, g.at[fy, pl.ds(half, half)], g.at[fy, pl.ds(half, half)], fx)
    s5 = gpush(5, g.at[fy], g.at[fy], mate)
    s3.wait_recv()
    block(fx, 1)
    s4.wait_recv()
    s6.wait_recv()
    s7 = gpush(7, g.at[fd], g.at[fd], mate)
    s5.wait_recv()
    block(fy, 2)
    s7.wait_recv()
    encode(fd)
    for copy in early:
        copy.wait_recv()
    for t in range(PAIRS + 8):
        for pair in range(PAIRS):
            s = t - pair
            if 0 <= s <= 8:
                if s == 0:
                    multiply(fd, pair)
                for h in range(2):
                    stage(s, 2 * pair + h)
    for copy in stores:
        copy.wait()
    for copy in [s0, s1, s2, s3, s4, s5, s6, s7] + early:
        copy.wait_send()
    for key, copy in live.items():
        if key[0] == "out":
            copy.wait()
        else:
            copy.wait_send()


def grad_kernel(scale, low_ref, acts_ref, dec_ref, fg_ref, dg_ref):
    fg_ref[0] = lax.dot_general(
        low_ref[...], dec_ref[...], (((1,), (1,)), ((), ())),
        preferred_element_type=jnp.float32).astype(fg_ref.dtype)
    dg = lax.dot_general(
        acts_ref[...], low_ref[...], (((0,), (0,)), ((), ())),
        preferred_element_type=jnp.float32)
    dg_ref[0] = (dg * scale).astype(dg_ref.dtype)


def body(layers, sources, w_encode, b_encode, w_decode, b_decode, target):
    encoder, bias, decoder = w_encode[0], b_encode, w_decode[0]
    dim, feats_dev = encoder.shape
    tokens = target.shape[0]
    scale = 1.0 / math.sqrt(tokens)
    shard = sources.shape[1]
    rows = tokens // (layers * 8)
    width = dim // (2 * PAIRS)
    chunks = 2 * PAIRS
    vmem = pl.BlockSpec(memory_space=pltpu.VMEM)
    any_ = pl.BlockSpec(memory_space=pl.ANY)
    bf = jnp.bfloat16
    dma = pltpu.SemaphoreType.DMA
    error_out, acts, low = pl.pallas_call(
        functools.partial(fused_kernel, layers),
        out_shape=(
            jax.ShapeDtypeStruct((rows, dim), jnp.float32),
            jax.ShapeDtypeStruct((tokens, feats_dev), bf),
            jax.ShapeDtypeStruct((layers, 2, 2, 2, rows, dim), bf),
        ),
        in_specs=[vmem, any_, vmem, any_, vmem, any_],
        out_specs=(vmem, any_, any_),
        scratch_shapes=[
            pltpu.VMEM((8, shard, dim), bf),
            pltpu.VMEM((dim, feats_dev), bf),
            pltpu.VMEM((tokens, feats_dev), bf),
            pltpu.VMEM((feats_dev, dim), bf),
            pltpu.VMEM((rows, dim), bf),
            pltpu.VMEM((chunks, 2, 2, 2, layers, rows, width), bf),
            pltpu.VMEM((chunks, 2, 2, layers, rows, width), bf),
            pltpu.VMEM((chunks, 2, layers, rows, width), bf),
            pltpu.VMEM((chunks, layers, rows, width), bf),
            pltpu.VMEM((chunks, layers - 1, rows, width), bf),
            pltpu.VMEM((chunks, layers, 2, 2, 2, rows, width), bf),
            dma((8,)), dma((8,)), dma((3,)), dma((3,)),
            dma((6, chunks)), dma((6, chunks)),
            dma((2, chunks, layers - 1)), dma((2, chunks, layers - 1)),
            dma((8 + chunks,)),
        ],
        compiler_params=pltpu.CompilerParams(
            collective_id=0, has_side_effects=True, vmem_limit_bytes=LIMIT),
    )(sources[0], encoder, bias, decoder, b_decode, target)
    low = low.reshape(tokens, dim)
    tile = 512 if feats_dev % 512 == 0 else feats_dev
    feature_grad, decoder_grad = pl.pallas_call(
        functools.partial(grad_kernel, scale),
        grid=(feats_dev // tile,),
        out_shape=(
            jax.ShapeDtypeStruct((1, tokens, feats_dev), bf),
            jax.ShapeDtypeStruct((1, feats_dev, dim), bf),
        ),
        in_specs=[
            pl.BlockSpec((tokens, dim), lambda i: (0, 0)),
            pl.BlockSpec((tokens, tile), lambda i: (0, i)),
            pl.BlockSpec((tile, dim), lambda i: (i, 0)),
        ],
        out_specs=(
            pl.BlockSpec((1, tokens, tile), lambda i: (0, 0, i)),
            pl.BlockSpec((1, tile, dim), lambda i: (0, i, 0)),
        ),
        compiler_params=pltpu.CompilerParams(vmem_limit_bytes=LIMIT),
    )(low, acts, decoder)
    return (error_out, feature_grad, decoder_grad)


def plain(sources, w_encode, b_encode, w_decode, b_decode, target):
    tok = lax.all_gather(sources[0], "feat", axis=0, tiled=True)
    pre = jnp.dot(tok, w_encode[0], preferred_element_type=jnp.float32) + b_encode[0]
    acts = jnp.maximum(pre, 0.0).astype(jnp.bfloat16)
    tokens = acts.shape[0]
    decoder = w_decode[0]
    rows = tokens // (lax.axis_size("layer") * lax.axis_size("feat"))
    own = lax.axis_index("layer") * lax.axis_size("feat") + lax.axis_index("feat")
    total = lax.psum(jnp.dot(acts, decoder, preferred_element_type=jnp.float32), ("layer", "feat"))
    error = total + b_decode - target.astype(jnp.float32)
    low = error.astype(jnp.bfloat16)
    grad_feat = lax.dot_general(
        low, decoder, (((1,), (1,)), ((), ())), preferred_element_type=jnp.float32)
    grad_dec = lax.dot_general(
        acts, low, (((0,), (0,)), ((), ())), preferred_element_type=jnp.float32)
    grad_dec = grad_dec * (1.0 / math.sqrt(tokens))
    return (lax.dynamic_slice_in_dim(error, own * rows, rows, 0),
            grad_feat.astype(jnp.bfloat16)[None], grad_dec.astype(jnp.bfloat16)[None])


def solution(mesh):
    layers, feats = mesh.shape["layer"], mesh.shape["feat"]
    placed = (
        P("layer", "feat", None),
        P("layer", None, "feat"),
        P("layer", "feat"),
        P("layer", "feat", None),
        P(),
        P(),
    )

    def run(*args):
        tokens, dim = args[5].shape
        fits = feats == 8 and layers == 4 and tokens % (layers * feats * 16) == 0 and dim % (PAIRS * 256) == 0
        chosen = functools.partial(body, layers) if fits else plain
        return jax.shard_map(
            chosen,
            mesh=mesh,
            in_specs=placed,
            out_specs=(P(("layer", "feat"), None), P("layer", None, "feat"),
                       P("layer", "feat", None)),
            check_vma=False,
        )(*args)

    return run
```
